128 devices in a mesh: dp: 2 (over y_hi), ctx: 16 (over x, z), tensor: 4 (over y_lo, core).
Axes of the slice: x: 4, y: 4 (y_hi: 2, y_lo: 2; y = y_hi * 2 + y_lo), z: 4, core: 2. Of those that a mesh axis runs over, the one named last changes fastest.
Arguments:
- values: bfloat16 [2, 4096, 4096], P('dp', 'ctx', 'tensor'), may hold values from -6 to 6
- b_proj: bfloat16 [2, 4096, 128], P('dp', 'ctx'), may hold values from -0.1875 to 0.1875
- c_proj: bfloat16 [2, 4096, 128], P('dp', 'ctx'), may hold values from -0.52734375 to 0.52734375
- step_sizes: float32 [2, 64, 4096], P('dp', 'tensor', 'ctx'), may hold values from 0.5 to 2
- decay_rates: float32 [64], P('tensor'), may hold values from 0.05 to 60
- skip_gain: float32 [64], P('tensor'), may hold values from 0.5 to 1.5
- w_out: bfloat16 [4096, 4096], P(None, 'tensor'), may hold values from -0.09375 to 0.09375
- d_out: bfloat16 [2, 4096, 4096], P('dp', 'ctx'), may hold values from -6 to 6
Outputs:
- d_values: bfloat16 [2, 4096, 4096], P('dp', 'ctx', 'tensor')
- d_b: float32 [2, 4096, 128], P('dp', 'ctx')
- d_c: float32 [2, 4096, 128], P('dp', 'ctx')
- d_steps: float32 [2, 64, 4096], P('dp', 'tensor', 'ctx')
- d_rates: float32 [64], P('tensor')
- d_skip: float32 [64], P('tensor')
- d_w: float32 [4096, 4096], P(('dp', 'ctx'), 'tensor')
The draws below stay inside these ranges and needn't reach their ends.
All inputs are finite; a program needn't handle non-finite values.
Results may differ from the reference program's by a relative error of at most 0.006.
Values sent between devices are 32-bit elements; how exact they have to be, the bound alone decides.
No kernel may reach another device: no remote copies, remote signals or barrier semaphores. Data moves between devices by JAX's collectives and lax.ppermute only.
A program may use at most 128 MiB of HBM per device.

```python
import math
import jax
import jax.numpy as jnp
from jax import lax

D = 4096
HEADS = 64
HEAD_DIM = 64
STATE = 128
INNER = 4096
SEQ = 4096
BATCH = 2


def with_spikes(values, own_key, source, target, parts, factor):
    def block_of(axis_at):
        return (jnp.arange(values.shape[axis_at]) // (values.shape[axis_at] // parts)).reshape((-1,) + (1,) * (values.ndim - 1 - axis_at))

    near = jax.random.permutation(own_key, parts)[block_of(target)]
    other_side = (block_of(target) + parts // 2) % parts
    return jnp.where((block_of(source) == near) | (block_of(source) == other_side), factor * values, values)


def shard_levels(stream_key, shape, cuts, low, high):
    gain, own = 1.0, jax.random.fold_in(stream_key, 6)
    for dim, shards_of in cuts:
        draws = jnp.exp(jax.random.uniform(jax.random.fold_in(own, dim), (shards_of,), jnp.float32, low / len(cuts), high / len(cuts)))
        gain = gain * jnp.repeat(draws, shape[dim] // shards_of).reshape([-1 if axis == dim else 1 for axis in range(len(shape))])
    return gain


def centred(stream_key, dims, scale, bound, shards=(), kind=jnp.bfloat16):
    gain = shard_levels(stream_key, dims, shards, -0.22, 0.18) if shards else 1.0
    array = jax.random.normal(stream_key, dims, jnp.float32) * scale * gain
    return jnp.minimum(jnp.maximum(array, -bound), bound).astype(kind)


def heavy_noise(stream_key, extent, deviation, limit, cuts, heavy, kind=jnp.bfloat16):
    drawn = deviation * jax.random.normal(stream_key, extent, jnp.float32)
    if cuts:
        drawn = drawn * shard_levels(stream_key, extent, cuts, -0.22, 0.18)
    return jnp.clip(with_spikes(drawn, jax.random.fold_in(stream_key, 3), *heavy), -limit, limit).astype(kind)


def setup_inputs(seed: int = 0) -> dict:
    key_of = jax.random.split(jax.random.key(seed), 9)
    return {
        "values": centred(key_of[0], (BATCH, SEQ, INNER), 1.0, 6.0, ((0, 2), (1, 16), (2, 4))),
        "b_proj": centred(key_of[1], (BATCH, SEQ, STATE), (2 * SEQ ** -0.5), 0.1875, ((0, 2), (1, 16))),
        "c_proj": centred(key_of[2], (BATCH, SEQ, STATE), (STATE ** -0.5), 0.52734375, ((0, 2), (1, 16))),
        "step_sizes": jnp.clip(jnp.exp(math.log(2.0) - 1.3862944 * jax.random.uniform(key_of[3], (BATCH, HEADS, SEQ), jnp.float32) ** shard_levels(key_of[3], (BATCH, HEADS, SEQ), ((0, 2), (1, 4), (2, 16)), -0.2, 0.2)), 0.5, 2.0),
        "decay_rates": jnp.clip(jnp.exp(math.log(60.0) - 7.090077 * jax.random.uniform(key_of[4], (HEADS,), jnp.float32) ** shard_levels(key_of[4], (HEADS,), ((0, 4),), -0.2, 0.2)), 0.05, 60.0),
        "skip_gain": jnp.clip(0.5 + 1.0 * jax.random.uniform(key_of[5], (HEADS,), jnp.float32) ** shard_levels(key_of[5], (HEADS,), ((0, 4),), -0.2, 0.2), 0.5, 1.5),
        "w_out": centred(key_of[6], (D, INNER), INNER ** -0.5, 0.09375, ((1, 4),)),
        "d_out": heavy_noise(key_of[7], (BATCH, SEQ, D), 1.0, 6.0, ((0, 2), (1, 16)), (1, 2, 16, 2.0)),
    }


high = lax.Precision.HIGHEST

def run_blocks(chan_vals, b_rows, c_rows, step_rows, rates, gains, start_state, length):
    total_len = chan_vals.shape[0]
    heads_here = chan_vals.shape[1]
    head_width = chan_vals.shape[2]
    state_width = b_rows.shape[1]
    block = min(256, total_len)
    nblocks = total_len // block
    vals_blk = chan_vals.reshape(nblocks, block, heads_here, head_width)
    b_blk = b_rows.reshape(nblocks, block, state_width)
    c_blk = c_rows.reshape(nblocks, block, state_width)
    step_blk = step_rows.reshape(heads_here, nblocks, block).transpose(1, 0, 2)
    position = jnp.arange(block)
    lower = position[:, None] >= position[None, :]

    def advance(state, pieces):
        vals_one, b_one, c_one, step_one = pieces
        logdecay = -step_one * rates[:, None] / length
        running = jnp.cumsum(logdecay, axis=1)
        between = running[:, :, None] - running[:, None, :]
        weights = jnp.exp(jnp.where(lower[None], between, -jnp.inf))
        intersection = jnp.einsum('in,jn->ij', c_one, b_one, precision=high)
        mixing = weights * intersection[None] * step_one[:, None, :]
        inside = jnp.einsum('hij,jhp->ihp', mixing, vals_one, precision=high)
        carried = jnp.exp(running).T[:, :, None] * jnp.einsum('in,hpn->ihp', c_one, state, precision=high)
        output = inside + carried + gains[None, :, None] * vals_one
        tail = jnp.exp(running[:, -1:] - running) * step_one
        fresh = jnp.einsum('hj,jhp,jn->hpn', tail, vals_one, b_one, precision=high)
        new_state = jnp.exp(running[:, -1])[:, None, None] * state + fresh
        return (new_state, output)
    end_state, outputs = lax.scan(jax.checkpoint(advance), start_state, (vals_blk, b_blk, c_blk, step_blk))
    return (outputs.reshape(total_len, heads_here, head_width), end_state)

def reference(values, b_proj, c_proj, step_sizes, decay_rates, skip_gain, w_out, d_out):

    def forward(vals, b_all, c_all, steps_all, rates, gains):

        def single(vals_one, b_one, c_one, steps_one):
            zero_state = jnp.zeros((HEADS, HEAD_DIM, STATE), jnp.float32)
            mixed, _ = run_blocks(vals_one.reshape(SEQ, HEADS, HEAD_DIM), b_one, c_one, steps_one, rates, gains, zero_state, SEQ)
            return mixed.reshape(SEQ, INNER)
        return jax.vmap(single)(vals, b_all, c_all, steps_all)
    mixed, pullback = jax.vjp(forward, values.astype(jnp.float32), b_proj.astype(jnp.float32), c_proj.astype(jnp.float32), step_sizes, decay_rates, skip_gain)
    mixed_bf = mixed.astype(jnp.bfloat16)
    upstream = jnp.stack([jnp.dot(d_out[index], w_out, preferred_element_type=jnp.float32) for index in range(BATCH)]).astype(jnp.bfloat16)
    d_w = jnp.zeros((D, INNER), jnp.float32)
    for index in range(BATCH):
        d_w = d_w + jnp.dot(d_out[index].T, mixed_bf[index], preferred_element_type=jnp.float32)
    grad_vals, grad_b, grad_c, grad_steps, grad_rates, grad_skip = pullback(upstream.astype(jnp.float32))
    return (grad_vals.astype(jnp.bfloat16), grad_b, grad_c, grad_steps, grad_rates, grad_skip, d_w)
```

```python
import functools

import jax
import jax.numpy as jnp
from jax import lax
from jax.experimental import pallas as pl
from jax.experimental.pallas import tpu as pltpu
from jax.sharding import PartitionSpec as P

F32 = jnp.float32
BF16 = jnp.bfloat16
NEG = -1e30
SIDE = 4


def dot(a, b, ca=1, cb=0):
    return lax.dot_general(a, b, (((ca,), (cb,)), ((), ())), preferred_element_type=F32)


def call(kernel, outs, name, scratch=(), scalars=0, flops=0, nbytes=0):
    vmem = pl.BlockSpec(memory_space=pltpu.VMEM)

    def run(*args):
        specs = [pl.BlockSpec(memory_space=pltpu.SMEM)] * scalars + [vmem] * (len(args) - scalars)
        return pl.pallas_call(
            kernel,
            out_shape=outs,
            in_specs=specs,
            out_specs=jax.tree.map(lambda _: vmem, outs),
            scratch_shapes=list(scratch),
            compiler_params=pltpu.CompilerParams(vmem_limit_bytes=56 * 1024 * 1024),
            cost_estimate=pl.CostEstimate(flops=flops, bytes_accessed=nbytes, transcendentals=0),
            name=name,
        )(*args)

    return run


def scan_lanes(x, reverse=False):
    n = x.shape[1]
    lane = lax.broadcasted_iota(jnp.int32, x.shape, 1)
    k = 1
    while k < n:
        if reverse:
            x = x + jnp.where(lane < n - k, pltpu.roll(x, n - k, 1), 0.0)
        else:
            x = x + jnp.where(lane >= k, pltpu.roll(x, k, 1), 0.0)
        k *= 2
    return x


def prep_kernel(pos, d_ref, z1, z2, z3, x1, x2, x3, oz, ox):
    dp, x, z, core = pos[0], pos[1], pos[2], pos[3]

    def column(d, xx, zz):
        at = (d * SIDE + lax.rem(xx, SIDE)) * SIDE + lax.rem(zz, SIDE)
        return d_ref[:, pl.ds(pl.multiple_of(at * 128, 128), 128)]

    mine = lax.rem(dp + core, 2)
    for k, (zr, xr) in enumerate(((z1, x1), (z2, x2), (z3, x3)), 1):
        for r in range(SIDE):
            cols = slice(r * 128, (r + 1) * 128)
            zr[:, cols] = column(mine, x + r, z + k).astype(F32)
            xr[:, cols] = column(mine, x + k, z + r).astype(F32)
    for kd in range(2):
        d = lax.rem(dp + kd, 2)
        for r in range(SIDE):
            cols = slice(r * 128, (r + 1) * 128)
            oz[kd, :, cols] = column(d, x + r, z)
            ox[kd, :, cols] = column(d, x, z + r)


def ends_kernel(v_ref, b_ref, s_ref, r_ref, vt_ref, end_ref, run_ref, *, length):
    heads, tokens = s_ref.shape
    width = v_ref.shape[1] // heads
    run = scan_lanes(s_ref[...] * (r_ref[...] * (-1.0 / length)))
    run_ref[...] = run
    last = run[:, tokens - 1 :]
    tail = jnp.exp(last - run) * s_ref[...]
    total = jnp.exp(last)
    b = b_ref[...]
    per = 128 // width
    for h in range(0, heads, per):
        vt = v_ref[:, h * width : (h + per) * width].astype(F32).T
        vt_ref[h * width : (h + per) * width, :] = vt.astype(BF16)
        for k in range(per):
            scaled = vt[k * width : (k + 1) * width] * tail[h + k : h + k + 1]
            end_ref[h + k, :width, :] = dot(scaled.astype(BF16), b)
            end_ref[h + k, width:, :] = jnp.broadcast_to(total[h + k : h + k + 1], (8, 128))


def before_kernel(e_ref, o_ref, keep_ref):
    shards, rows, _ = o_ref.shape
    state = jnp.zeros(o_ref.shape[1:], F32)
    for k in range(shards):
        o_ref[k] = state
        decay = e_ref[k, rows:, :]
        keep_ref[k] = decay
        if k < shards - 1:
            state = state * decay[0:1] + e_ref[k, :rows, :]


def after_kernel(e_ref, keep_ref, o_ref):
    shards = o_ref.shape[0]
    state = jnp.zeros(o_ref.shape[1:], F32)
    for k in reversed(range(shards)):
        o_ref[k] = state
        if k:
            state = state * keep_ref[k, 0:1] + e_ref[k]


def columns_of(run, wide_ref):
    heads, tokens = run.shape
    turned = jnp.concatenate([run, jnp.zeros((128 - heads, tokens), F32)], 0).T
    for h in range(heads):
        wide_ref[h] = jnp.broadcast_to(turned[:, h : h + 1], (tokens, 128))


def weights_of(wide, row, steps, tokens):
    i = lax.broadcasted_iota(jnp.int32, (tokens, tokens), 0)
    j = lax.broadcasted_iota(jnp.int32, (tokens, tokens), 1)
    between = jnp.concatenate([wide] * (tokens // 128), 1) - row
    return jnp.exp(jnp.where(i >= j, between, NEG)) * steps


def mix_kernel(g_ref, vt_ref, b_ref, c_ref, s_ref, run_ref, sin_ref, ma_ref, mb_ref, wide_ref, g2_ref):
    heads, tokens = s_ref.shape
    width = vt_ref.shape[0] // heads
    columns_of(run_ref[...], wide_ref)
    g2_ref[...] = dot(c_ref[...], b_ref[...], 1, 1)
    half = heads // 2

    def head(h, out_ref, base):
        row = run_ref[pl.ds(h, 1), :]
        mix = (weights_of(wide_ref[h], row, s_ref[pl.ds(h, 1), :], tokens) * g2_ref[...]).astype(BF16)
        at = pl.ds(pl.multiple_of(h * width, width), width)
        v = vt_ref[at, :]
        inside = dot(v, mix, 1, 1)
        carried = dot(sin_ref[h].astype(BF16), c_ref[...], 1, 1) * jnp.exp(row)
        to = pl.ds(pl.multiple_of((h - base) * width, width), width)
        out_ref[to, :] = inside + carried + g_ref[h] * v.astype(F32)

    lax.fori_loop(0, half, lambda h, _: head(h, ma_ref, 0), None, unroll=2)
    lax.fori_loop(half, heads, lambda h, _: head(h, mb_ref, half), None, unroll=2)


def grad_ends_kernel(ut_ref, c_ref, run_ref, o_ref):
    heads, width, _ = o_ref.shape
    grow = jnp.exp(run_ref[...])
    c = c_ref[...]
    for h in range(heads):
        scaled = ut_ref[h * width : (h + 1) * width, :].astype(F32) * grow[h : h + 1]
        o_ref[h] = dot(scaled.astype(BF16), c)


def back_kernel(
    g_ref, ut_ref, vt_ref, b_ref, c_ref, s_ref, run_ref, r_ref, sin_ref, gs_ref, ma_ref, mb_ref,
    dv_ref, dbc_ref, ds_ref, small_ref,
    wide_ref, g2_ref, ct_ref, bt_ref, ue_ref, vw_ref, r1_ref, q_ref, add_ref, skip_ref, dbt_ref, dct_ref, dvt_ref,
    *, length,
):
    heads, tokens = s_ref.shape
    width = vt_ref.shape[0] // heads
    half = heads // 2
    columns_of(run_ref[...], wide_ref)
    g2_ref[...] = dot(c_ref[...], b_ref[...], 1, 1)
    ct_ref[...] = c_ref[...].astype(F32).T.astype(BF16)
    bt_ref[...] = b_ref[...].astype(F32).T.astype(BF16)
    dbt_ref[...] = jnp.zeros_like(dbt_ref)
    dct_ref[...] = jnp.zeros_like(dct_ref)

    def head(h, mixed_ref, base):
        row = run_ref[pl.ds(h, 1), :]
        steps = s_ref[pl.ds(h, 1), :]
        last = row[:, tokens - 1 :]
        at = pl.ds(pl.multiple_of(h * width, width), width)
        v, u = vt_ref[at, :], ut_ref[at, :]
        vf, uf = v.astype(F32), u.astype(F32)
        weights = weights_of(wide_ref[h], row, steps, tokens)
        mix = (weights * g2_ref[...]).astype(BF16)
        pair = dot(u, v, 0, 0)
        dg = (pair * weights).astype(BF16)
        dct_ref[...] += dot(bt_ref[...], dg, 1, 1)
        dbt_ref[...] += dot(ct_ref[...], dg, 1, 0)
        tail = jnp.exp(last - row) * steps
        ue_ref[at, :] = (uf * jnp.exp(row)).astype(BF16)
        vw_ref[at, :] = (vf * tail).astype(BF16)
        gs = gs_ref[h]
        far = dot(gs.astype(BF16), bt_ref[...]) * tail
        near = dot(u, mix)
        both = near + far
        gain = g_ref[h]
        dvt_ref[at, :] = both + gain * uf
        out = mixed_ref[pl.ds(pl.multiple_of((h - base) * width, width), width), :] - gain * vf
        r1_ref[pl.ds(h, 1), :] = jnp.sum(uf * out, 0, keepdims=True)
        q_ref[pl.ds(h, 1), :] = jnp.sum(vf * both, 0, keepdims=True)
        kept = jnp.sum(sin_ref[h] * gs, 0, keepdims=True) * jnp.exp(last)
        add_ref[pl.ds(h, 1), :] = jnp.sum(vf * far, 0, keepdims=True) + jnp.concatenate(
            [kept, jnp.zeros((1, tokens - 128), F32)], 1
        )
        skip_ref[pl.ds(h, 1), :] = jnp.sum(uf * vf, 0, keepdims=True)

    lax.fori_loop(0, half, lambda h, _: head(h, ma_ref, 0), None, unroll=2)
    lax.fori_loop(half, heads, lambda h, _: head(h, mb_ref, half), None, unroll=2)

    states = sin_ref.shape[0] * sin_ref.shape[1]
    sin_t = sin_ref[...].reshape(states, 128).T.astype(BF16)
    gs_t = gs_ref[...].reshape(states, 128).T.astype(BF16)
    dbc_ref[0] = (dbt_ref[...] + dot(gs_t, vw_ref[...])).T
    dbc_ref[1] = (dct_ref[...] + dot(sin_t, ue_ref[...])).T
    for k in range(0, heads * width, 128):
        dv_ref[:, k : k + 128] = dvt_ref[k : k + 128, :].T.astype(BF16)
    dlog = scan_lanes(r1_ref[...] - q_ref[...], reverse=True) + jnp.sum(add_ref[...], 1, keepdims=True)
    s = s_ref[...]
    ds_ref[...] = q_ref[...] / s - dlog * (r_ref[...] * (1.0 / length))
    rates = jnp.sum(s * dlog, 1, keepdims=True) * (-1.0 / length)
    skips = jnp.sum(skip_ref[...], 1, keepdims=True)
    lane = lax.broadcasted_iota(jnp.int32, (heads, 128), 1)
    small_ref[...] = jnp.where(lane == 0, rates, jnp.where(lane == 1, skips, 0.0))


def grad_w_kernel(core, m0, m1, m2, m3, own, d1, d2, d3, e_ref, o0, o1, o2, o3):
    outs = (o0, o1, o2, o3)
    ms = [m[...].astype(BF16) for m in (m0, m1, m2, m3)]
    ds = (d1, d2, d3)
    me = core[0]
    for kd in range(2):
        at = me if kd == 0 else 1 - me
        acc = dot(ms[0], own[at])
        for k in range(3):
            piece = ds[k][...] if kd == 0 else e_ref[k]
            acc += dot(ms[k + 1], piece.astype(BF16))
        for r in range(SIDE):
            outs[r][at] = acc[:, r * 128 : (r + 1) * 128]


def gather_sum_kernel(a0, a1, a2, a3, b0, b1, b2, b3, keep_ref, send_ref):
    n = a0.shape[1]
    for at, (w, x, y, z) in ((0, (a0, a1, a2, a3)), (n, (b0, b1, b2, b3))):
        keep_ref[at : at + n, :] = w[0] + x[0] + y[0] + z[0]
        send_ref[at : at + n, :] = w[1] + x[1] + y[1] + z[1]


def finish_kernel(a_ref, b_ref, o_ref):
    o_ref[...] = (a_ref[...] + b_ref[...]).T


def body(values, b_proj, c_proj, step_sizes, decay_rates, skip_gain, w_out, d_out):
    tokens, channels = values.shape[1:]
    state = b_proj.shape[2]
    heads = decay_rates.shape[0]
    width = channels // heads
    shards = lax.axis_size("ctx")
    length = tokens * shards
    half = channels // 2
    sds = jax.ShapeDtypeStruct

    place = lax.axis_index("ctx")
    dp = lax.axis_index("dp")
    core = lax.rem(lax.axis_index("tensor"), 2)
    pos = jnp.stack([dp, place // SIDE, lax.rem(place, SIDE), core]).astype(jnp.int32)

    def shift(value, dx, dz):
        pairs = [
            (x * SIDE + z, ((x + dx) % SIDE) * SIDE + (z + dz) % SIDE)
            for x in range(SIDE)
            for z in range(SIDE)
        ]
        return lax.ppermute(value, "ctx", pairs)

    def other_core(value):
        return lax.ppermute(value, "tensor", [(0, 1), (1, 0), (2, 3), (3, 2)])

    def other_chip(value):
        return lax.ppermute(value, "tensor", [(0, 2), (2, 0), (1, 3), (3, 1)])

    def other_dp(value):
        return lax.ppermute(value, "dp", [(0, 1), (1, 0)])

    def spread(value):
        return lax.all_to_all(value, "ctx", 0, 0, tiled=True)

    v, b, c, steps, cot = values[0], b_proj[0], c_proj[0], step_sizes[0], d_out[0]
    rates = decay_rates[:, None]

    piece = sds((tokens, 4 * 128), F32)
    own = sds((2, tokens, 4 * 128), BF16)
    z1, z2, z3, x1, x2, x3, own_z, own_x = call(
        prep_kernel, (piece,) * 6 + (own, own), "prep", scalars=1, nbytes=7 << 20
    )(pos, cot)
    vt, ends, run = call(
        functools.partial(ends_kernel, length=length),
        (sds((channels, tokens), BF16), sds((heads, width + 8, state), F32), sds((heads, tokens), F32)),
        "ends",
        nbytes=2 << 20,
        flops=1 << 26,
    )(v, b, steps, rates)
    z1, z2, z3 = shift(z1, 0, 1), shift(z2, 0, 2), shift(z3, 0, 3)
    x1, x2, x3 = shift(x1, 1, 0), shift(x2, 2, 0), shift(x3, 3, 0)

    before, keep = call(
        before_kernel, (sds((shards, width, state), F32), sds((shards, 8, state), F32)), "before", nbytes=1 << 20
    )(spread(ends))
    state_in = spread(before)

    wide = pltpu.VMEM((heads, tokens, 128), F32)
    square = pltpu.VMEM((tokens, tokens), F32)
    mixed_a, mixed_b = call(
        mix_kernel, (sds((half, tokens), F32),) * 2, "mix", (wide, square), scalars=1, nbytes=4 << 20, flops=1 << 28
    )(skip_gain, vt, b, c, steps, run, state_in)

    a1, a2, a3 = shift(mixed_a, 0, 1), shift(mixed_a, 0, 2), shift(mixed_a, 0, 3)
    b1, b2, b3 = shift(mixed_b, 1, 0), shift(mixed_b, 2, 0), shift(mixed_b, 3, 0)

    swapped = other_core(jnp.stack([z1, z2, z3, x1, x2, x3]))
    up_t = lax.dot_general(w_out, cot, (((0,), (1,)), ((), ())), preferred_element_type=F32).astype(BF16)
    grad_ends = call(grad_ends_kernel, sds((heads, width, state), F32), "grad_ends", nbytes=2 << 20, flops=1 << 26)(
        up_t, c, run
    )
    after = call(after_kernel, sds((shards, width, state), F32), "after", nbytes=1 << 20)(spread(grad_ends), keep)
    grad_out = spread(after)

    out = (sds((2, half, 128), F32),) * 4
    flops = 2 * half * 4 * tokens * 1024
    pa = call(grad_w_kernel, out, "grad_w_a", scalars=1, flops=flops, nbytes=8 << 20)(
        core[None].astype(jnp.int32), mixed_a, a1, a2, a3, own_z, z1, z2, z3, swapped[:3]
    )
    pb = call(grad_w_kernel, out, "grad_w_b", scalars=1, flops=flops, nbytes=8 << 20)(
        core[None].astype(jnp.int32), mixed_b, b1, b2, b3, own_x, x1, x2, x3, swapped[3:]
    )
    ra = [pa[0]] + [shift(pa[k], k, 0) for k in range(1, SIDE)]
    rb = [pb[0]] + [shift(pb[k], 0, k) for k in range(1, SIDE)]

    dv, dbc, dsteps, small = call(
        functools.partial(back_kernel, length=length),
        (
            sds((tokens, channels), BF16),
            sds((2, tokens, state), F32),
            sds((heads, tokens), F32),
            sds((heads, 128), F32),
        ),
        "back",
        (
            wide, square, pltpu.VMEM((state, tokens), BF16), pltpu.VMEM((state, tokens), BF16),
            pltpu.VMEM((channels, tokens), BF16), pltpu.VMEM((channels, tokens), BF16),
            pltpu.VMEM((heads, tokens), F32), pltpu.VMEM((heads, tokens), F32),
            pltpu.VMEM((heads, tokens), F32), pltpu.VMEM((heads, tokens), F32),
            pltpu.VMEM((state, tokens), F32), pltpu.VMEM((state, tokens), F32),
            pltpu.VMEM((channels, tokens), F32),
        ),
        scalars=1,
        flops=1 << 30,
        nbytes=6 << 20,
    )(skip_gain, up_t, vt, b, c, steps, run, rates, state_in, grad_out, mixed_a, mixed_b)

    dbc = dbc + other_core(dbc)
    dbc = dbc + other_chip(dbc)
    small = spread(jnp.broadcast_to(small[None], (shards,) + small.shape)).sum(0)
    small = small + other_dp(small)

    kept, sent = call(gather_sum_kernel, (sds((channels, 128), F32),) * 2, "gather_sum", nbytes=5 << 20)(*ra, *rb)
    d_w = call(finish_kernel, sds((128, channels), F32), "finish", nbytes=2 << 20)(kept, other_dp(sent))
    return (dv[None], dbc[0][None], dbc[1][None], dsteps[None], small[:, 0], small[:, 1], d_w)


def solution(mesh):
    return jax.shard_map(
        body,
        mesh=mesh,
        in_specs=(
            P("dp", "ctx", "tensor"),
            P("dp", "ctx", None),
            P("dp", "ctx", None),
            P("dp", "tensor", "ctx"),
            P("tensor"),
            P("tensor"),
            P(None, "tensor"),
            P("dp", "ctx", None),
        ),
        out_specs=(
            P("dp", "ctx", "tensor"),
            P("dp", "ctx", None),
            P("dp", "ctx", None),
            P("dp", "tensor", "ctx"),
            P("tensor"),
            P("tensor"),
            P(("dp", "ctx"), "tensor"),
        ),
        check_vma=False,
    )
```

```python
import functools

import jax
import jax.numpy as jnp
from jax import lax
from jax.experimental import pallas as pl
from jax.experimental.pallas import tpu as pltpu
from jax.sharding import PartitionSpec as P

F32 = jnp.float32
BF16 = jnp.bfloat16
NEG = -1e30
SIDE = 4


def dot(a, b, ca=1, cb=0):
    return lax.dot_general(a, b, (((ca,), (cb,)), ((), ())), preferred_element_type=F32)


def call(kernel, outs, name, scratch=(), scalars=0, flops=0, nbytes=0):
    vmem = pl.BlockSpec(memory_space=pltpu.VMEM)

    def run(*args):
        specs = [pl.BlockSpec(memory_space=pltpu.SMEM)] * scalars + [vmem] * (len(args) - scalars)
        return pl.pallas_call(
            kernel,
            out_shape=outs,
            in_specs=specs,
            out_specs=jax.tree.map(lambda _: vmem, outs),
            scratch_shapes=list(scratch),
            compiler_params=pltpu.CompilerParams(vmem_limit_bytes=56 * 1024 * 1024),
            cost_estimate=pl.CostEstimate(flops=flops, bytes_accessed=nbytes, transcendentals=0),
            name=name,
        )(*args)

    return run


def scan_lanes(x, reverse=False):
    n = x.shape[1]
    lane = lax.broadcasted_iota(jnp.int32, x.shape, 1)
    k = 1
    while k < n:
        if reverse:
            x = x + jnp.where(lane < n - k, pltpu.roll(x, n - k, 1), 0.0)
        else:
            x = x + jnp.where(lane >= k, pltpu.roll(x, k, 1), 0.0)
        k *= 2
    return x


def prep_kernel(pos, d_ref, z1, z2, z3, x1, x2, x3, oz, ox):
    dp, x, z, core = pos[0], pos[1], pos[2], pos[3]

    def column(d, xx, zz):
        at = (d * SIDE + lax.rem(xx, SIDE)) * SIDE + lax.rem(zz, SIDE)
        return d_ref[:, pl.ds(pl.multiple_of(at * 128, 128), 128)]

    mine = lax.rem(dp + core, 2)
    for k, (zr, xr) in enumerate(((z1, x1), (z2, x2), (z3, x3)), 1):
        for r in range(SIDE):
            cols = slice(r * 128, (r + 1) * 128)
            zr[:, cols] = column(mine, x + r, z + k).astype(F32)
            xr[:, cols] = column(mine, x + k, z + r).astype(F32)
    for kd in range(2):
        d = lax.rem(dp + kd, 2)
        for r in range(SIDE):
            cols = slice(r * 128, (r + 1) * 128)
            oz[kd, :, cols] = column(d, x + r, z)
            ox[kd, :, cols] = column(d, x, z + r)


def ends_kernel(ut_ref, v_ref, b_ref, c_ref, s_ref, r_ref, vt_ref, end_ref, run_ref, *, length):
    heads, tokens = s_ref.shape
    width = v_ref.shape[1] // heads
    run = scan_lanes(s_ref[...] * (r_ref[...] * (-1.0 / length)))
    run_ref[...] = run
    last = run[:, tokens - 1 :]
    grow = jnp.exp(run)
    tail = jnp.exp(last - run) * s_ref[...]
    total = jnp.exp(last)
    b = b_ref[...]
    c = c_ref[...]
    per = 128 // width
    for h in range(0, heads, per):
        vt = v_ref[:, h * width : (h + per) * width].astype(F32).T
        vt_ref[h * width : (h + per) * width, :] = vt.astype(BF16)
        for k in range(per):
            at = h + k
            scaled = vt[k * width : (k + 1) * width] * tail[at : at + 1]
            end_ref[at, :width, :] = dot(scaled.astype(BF16), b)
            scaled = ut_ref[at * width : (at + 1) * width, :].astype(F32) * grow[at : at + 1]
            end_ref[at, width : 2 * width, :] = dot(scaled.astype(BF16), c)
            end_ref[at, 2 * width :, :] = jnp.broadcast_to(total[at : at + 1], (8, 128))


def across_kernel(e_ref, o_ref):
    shards, rows, _ = o_ref.shape
    width = rows // 2
    state = jnp.zeros((width, o_ref.shape[2]), F32)
    for k in range(shards):
        o_ref[k, :width, :] = state
        if k < shards - 1:
            state = state * e_ref[k, rows : rows + 1, :] + e_ref[k, :width, :]
    state = jnp.zeros((width, o_ref.shape[2]), F32)
    for k in reversed(range(shards)):
        o_ref[k, width:, :] = state
        if k:
            state = state * e_ref[k, rows : rows + 1, :] + e_ref[k, width:rows, :]


def columns_of(run, wide_ref):
    heads, tokens = run.shape
    turned = jnp.concatenate([run, jnp.zeros((128 - heads, tokens), F32)], 0).T
    for h in range(heads):
        wide_ref[h] = jnp.broadcast_to(turned[:, h : h + 1], (tokens, 128))


def weights_of(wide, row, steps, tokens):
    i = lax.broadcasted_iota(jnp.int32, (tokens, tokens), 0)
    j = lax.broadcasted_iota(jnp.int32, (tokens, tokens), 1)
    between = jnp.concatenate([wide] * (tokens // 128), 1) - row
    return jnp.exp(jnp.where(i >= j, between, NEG)) * steps


def mix_kernel(g_ref, vt_ref, b_ref, c_ref, s_ref, run_ref, st_ref, ma_ref, mb_ref, wide_ref, g2_ref):
    heads, tokens = s_ref.shape
    width = vt_ref.shape[0] // heads
    columns_of(run_ref[...], wide_ref)
    g2_ref[...] = dot(c_ref[...], b_ref[...], 1, 1)
    half = heads // 2

    def head(h, out_ref, base):
        row = run_ref[pl.ds(h, 1), :]
        mix = (weights_of(wide_ref[h], row, s_ref[pl.ds(h, 1), :], tokens) * g2_ref[...]).astype(BF16)
        at = pl.ds(pl.multiple_of(h * width, width), width)
        v = vt_ref[at, :]
        inside = dot(v, mix, 1, 1)
        carried = dot(st_ref[h, :width, :].astype(BF16), c_ref[...], 1, 1) * jnp.exp(row)
        to = pl.ds(pl.multiple_of((h - base) * width, width), width)
        out_ref[to, :] = inside + carried + g_ref[h] * v.astype(F32)

    lax.fori_loop(0, half, lambda h, _: head(h, ma_ref, 0), None, unroll=2)
    lax.fori_loop(half, heads, lambda h, _: head(h, mb_ref, half), None, unroll=2)


def back_kernel(
    g_ref, ut_ref, vt_ref, b_ref, c_ref, s_ref, run_ref, r_ref, st_ref, ma_ref, mb_ref,
    dv_ref, dbc_ref, ds_ref, small_ref,
    wide_ref, g2_ref, ct_ref, bt_ref, ue_ref, vw_ref, r1_ref, q_ref, add_ref, skip_ref, dbt_ref, dct_ref, dvt_ref,
    *, length,
):
    heads, tokens = s_ref.shape
    width = vt_ref.shape[0] // heads
    half = heads // 2
    columns_of(run_ref[...], wide_ref)
    g2_ref[...] = dot(c_ref[...], b_ref[...], 1, 1)
    ct_ref[...] = c_ref[...].astype(F32).T.astype(BF16)
    bt_ref[...] = b_ref[...].astype(F32).T.astype(BF16)
    dbt_ref[...] = jnp.zeros_like(dbt_ref)
    dct_ref[...] = jnp.zeros_like(dct_ref)

    def head(h, mixed_ref, base):
        row = run_ref[pl.ds(h, 1), :]
        steps = s_ref[pl.ds(h, 1), :]
        last = row[:, tokens - 1 :]
        at = pl.ds(pl.multiple_of(h * width, width), width)
        v, u = vt_ref[at, :], ut_ref[at, :]
        vf, uf = v.astype(F32), u.astype(F32)
        weights = weights_of(wide_ref[h], row, steps, tokens)
        mix = (weights * g2_ref[...]).astype(BF16)
        pair = dot(u, v, 0, 0)
        dg = (pair * weights).astype(BF16)
        dct_ref[...] += dot(bt_ref[...], dg, 1, 1)
        dbt_ref[...] += dot(ct_ref[...], dg, 1, 0)
        tail = jnp.exp(last - row) * steps
        ue_ref[at, :] = (uf * jnp.exp(row)).astype(BF16)
        vw_ref[at, :] = (vf * tail).astype(BF16)
        gs = st_ref[h, width:, :]
        far = dot(gs.astype(BF16), bt_ref[...]) * tail
        near = dot(u, mix)
        both = near + far
        gain = g_ref[h]
        dvt_ref[at, :] = both + gain * uf
        out = mixed_ref[pl.ds(pl.multiple_of((h - base) * width, width), width), :] - gain * vf
        r1_ref[pl.ds(h, 1), :] = jnp.sum(uf * out, 0, keepdims=True)
        q_ref[pl.ds(h, 1), :] = jnp.sum(vf * both, 0, keepdims=True)
        kept = jnp.sum(st_ref[h, :width, :] * gs, 0, keepdims=True) * jnp.exp(last)
        add_ref[pl.ds(h, 1), :] = jnp.sum(vf * far, 0, keepdims=True) + jnp.concatenate(
            [kept, jnp.zeros((1, tokens - 128), F32)], 1
        )
        skip_ref[pl.ds(h, 1), :] = jnp.sum(uf * vf, 0, keepdims=True)

    lax.fori_loop(0, half, lambda h, _: head(h, ma_ref, 0), None, unroll=2)
    lax.fori_loop(half, heads, lambda h, _: head(h, mb_ref, half), None, unroll=2)

    states = heads * width
    sin_t = st_ref[:, :width, :].reshape(states, 128).T.astype(BF16)
    gs_t = st_ref[:, width:, :].reshape(states, 128).T.astype(BF16)
    dbc_ref[0] = (dbt_ref[...] + dot(gs_t, vw_ref[...])).T
    dbc_ref[1] = (dct_ref[...] + dot(sin_t, ue_ref[...])).T
    for k in range(0, heads * width, 128):
        dv_ref[:, k : k + 128] = dvt_ref[k : k + 128, :].T.astype(BF16)
    dlog = scan_lanes(r1_ref[...] - q_ref[...], reverse=True) + jnp.sum(add_ref[...], 1, keepdims=True)
    s = s_ref[...]
    ds_ref[...] = q_ref[...] / s - dlog * (r_ref[...] * (1.0 / length))
    rates = jnp.sum(s * dlog, 1, keepdims=True) * (-1.0 / length)
    skips = jnp.sum(skip_ref[...], 1, keepdims=True)
    lane = lax.broadcasted_iota(jnp.int32, (heads, 128), 1)
    head_of = lax.broadcasted_iota(jnp.int32, (heads, 128), 0)
    packed = jnp.where(lane == head_of, rates, jnp.where(lane == head_of + heads, skips, 0.0))
    small_ref[...] = jnp.sum(packed, 0, keepdims=True)


def grad_w_kernel(core, m0, m1, m2, m3, own, d1, d2, d3, e1, e2, e3, o0, o1, o2, o3):
    outs = (o0, o1, o2, o3)
    ms = [m[...].astype(BF16) for m in (m0, m1, m2, m3)]
    ds = ((d1, d2, d3), (e1, e2, e3))
    me = core[0]
    for kd in range(2):
        at = me if kd == 0 else 1 - me
        acc = dot(ms[0], own[at])
        for k in range(3):
            acc += dot(ms[k + 1], ds[kd][k][...].astype(BF16))
        for r in range(SIDE):
            outs[r][at] = acc[:, r * 128 : (r + 1) * 128]


def gather_sum_kernel(a0, a1, a2, a3, keep_ref, send_ref):
    keep_ref[...] = a0[0] + a1[0] + a2[0] + a3[0]
    send_ref[...] = a0[1] + a1[1] + a2[1] + a3[1]


def finish_kernel(a0, a1, b0, b1, o_ref):
    n = a0.shape[0]
    o_ref[:, :n] = (a0[...] + a1[...]).T
    o_ref[:, n:] = (b0[...] + b1[...]).T


def body(values, b_proj, c_proj, step_sizes, decay_rates, skip_gain, w_out, d_out):
    tokens, channels = values.shape[1:]
    state = b_proj.shape[2]
    heads = decay_rates.shape[0]
    width = channels // heads
    shards = lax.axis_size("ctx")
    length = tokens * shards
    half = channels // 2
    sds = jax.ShapeDtypeStruct

    place = lax.axis_index("ctx")
    dp = lax.axis_index("dp")
    core = lax.rem(lax.axis_index("tensor"), 2)
    pos = jnp.stack([dp, place // SIDE, lax.rem(place, SIDE), core]).astype(jnp.int32)

    def shift(value, dx, dz):
        pairs = [
            (x * SIDE + z, ((x + dx) % SIDE) * SIDE + (z + dz) % SIDE)
            for x in range(SIDE)
            for z in range(SIDE)
        ]
        return lax.ppermute(value, "ctx", pairs)

    def other_core(value):
        return lax.ppermute(value, "tensor", [(0, 1), (1, 0), (2, 3), (3, 2)])

    def other_chip(value):
        return lax.ppermute(value, "tensor", [(0, 2), (2, 0), (1, 3), (3, 1)])

    def other_dp(value):
        return lax.ppermute(value, "dp", [(0, 1), (1, 0)])

    def spread(value):
        return lax.all_to_all(value, "ctx", 0, 0, tiled=True)

    v, b, c, steps, cot = values[0], b_proj[0], c_proj[0], step_sizes[0], d_out[0]
    rates = decay_rates[:, None]

    def later(value, *first):
        return lax.optimization_barrier((value,) + first)[0]

    piece = sds((tokens, 4 * 128), F32)
    own = sds((2, tokens, 4 * 128), BF16)
    z1, z2, z3, x1, x2, x3, own_z, own_x = call(
        prep_kernel, (piece,) * 6 + (own, own), "prep", scalars=1, nbytes=7 << 20
    )(pos, cot)
    z3, x3, z1, x1 = shift(z3, 0, 3), shift(x3, 3, 0), shift(z1, 0, 1), shift(x1, 1, 0)

    up_t = lax.dot_general(w_out, later(cot, own_z), (((0,), (1,)), ((), ())), preferred_element_type=F32).astype(BF16)
    vt, ends, run = call(
        functools.partial(ends_kernel, length=length),
        (sds((channels, tokens), BF16), sds((heads, 2 * width + 8, state), F32), sds((heads, tokens), F32)),
        "ends",
        nbytes=4 << 20,
        flops=1 << 27,
    )(up_t, v, b, c, steps, rates)
    z2, x2 = shift(later(z2, run), 0, 2), shift(later(x2, run), 2, 0)
    ends = later(ends, z1, z3, x1, x3)
    across = call(across_kernel, sds((shards, 2 * width, state), F32), "across", nbytes=2 << 20)(spread(ends))
    states = spread(across)
    sent = [z1, z2, z3, x1, x2, x3]

    wide = pltpu.VMEM((heads, tokens, 128), F32)
    square = pltpu.VMEM((tokens, tokens), F32)
    mixed_a, mixed_b = call(
        mix_kernel, (sds((half, tokens), F32),) * 2, "mix", (wide, square), scalars=1, nbytes=4 << 20, flops=1 << 28
    )(skip_gain, vt, b, c, steps, run, states)

    swapped = [other_core(p) for p in lax.optimization_barrier((*sent, across))[:6]]
    ready = lax.optimization_barrier((mixed_a, mixed_b, *swapped))
    mixed_a, mixed_b, swapped = ready[0], ready[1], ready[2:]
    b1, b3 = shift(mixed_b, 1, 0), shift(mixed_b, 3, 0)
    a1, a3, a2 = shift(mixed_a, 0, 1), shift(mixed_a, 0, 3), shift(mixed_a, 0, 2)

    dv, dbc, dsteps, small = call(
        functools.partial(back_kernel, length=length),
        (
            sds((tokens, channels), BF16),
            sds((2, tokens, state), F32),
            sds((heads, tokens), F32),
            sds((1, 128), F32),
        ),
        "back",
        (
            wide, square, pltpu.VMEM((state, tokens), BF16), pltpu.VMEM((state, tokens), BF16),
            pltpu.VMEM((channels, tokens), BF16), pltpu.VMEM((channels, tokens), BF16),
            pltpu.VMEM((heads, tokens), F32), pltpu.VMEM((heads, tokens), F32),
            pltpu.VMEM((heads, tokens), F32), pltpu.VMEM((heads, tokens), F32),
            pltpu.VMEM((state, tokens), F32), pltpu.VMEM((state, tokens), F32),
            pltpu.VMEM((channels, tokens), F32),
        ),
        scalars=1,
        flops=1 << 30,
        nbytes=6 << 20,
    )(skip_gain, up_t, vt, b, c, steps, run, rates, states, mixed_a, mixed_b)

    b2 = shift(later(mixed_b, b1, b3, small), 2, 0)
    small = spread(jnp.broadcast_to(small[None], (shards,) + small.shape)).sum(0)

    out = (sds((2, half, 128), F32),) * 4
    flops = 2 * half * 4 * tokens * 1024
    me = core[None].astype(jnp.int32)
    pa = call(grad_w_kernel, out, "grad_w_a", scalars=1, flops=flops, nbytes=8 << 20)(
        me, later(mixed_a, small), a1, a2, a3, own_z, *sent[:3], *swapped[:3]
    )
    ra = [pa[0]] + [shift(pa[k], k, 0) for k in range(1, SIDE)]
    pb = call(grad_w_kernel, out, "grad_w_b", scalars=1, flops=flops, nbytes=8 << 20)(
        me, later(mixed_b, pa[0]), b1, b2, b3, own_x, *sent[3:], *swapped[3:]
    )
    rb = [pb[0]] + [shift(pb[k], 0, k) for k in range(1, SIDE)]

    dbc = dbc + other_core(dbc)
    dbc = dbc + other_chip(dbc)
    small = small + other_dp(small)

    pair = (sds((half, 128), F32),) * 2
    kept_a, away_a = call(gather_sum_kernel, pair, "gather_sum_a", nbytes=3 << 20)(*ra)
    away_a = other_dp(away_a)
    kept_b, away_b = call(gather_sum_kernel, pair, "gather_sum_b", nbytes=3 << 20)(*rb)
    away_b = other_dp(away_b)
    d_w = call(finish_kernel, sds((128, channels), F32), "finish", nbytes=2 << 20)(kept_a, away_a, kept_b, away_b)
    return (dv[None], dbc[0][None], dbc[1][None], dsteps[None], small[0, :heads], small[0, heads : 2 * heads], d_w)


def solution(mesh):
    return jax.shard_map(
        body,
        mesh=mesh,
        in_specs=(
            P("dp", "ctx", "tensor"),
            P("dp", "ctx", None),
            P("dp", "ctx", None),
            P("dp", "tensor", "ctx"),
            P("tensor"),
            P("tensor"),
            P(None, "tensor"),
            P("dp", "ctx", None),
        ),
        out_specs=(
            P("dp", "ctx", "tensor"),
            P("dp", "ctx", None),
            P("dp", "ctx", None),
            P("dp", "tensor", "ctx"),
            P("tensor"),
            P("tensor"),
            P(("dp", "ctx"), "tensor"),
        ),
        check_vma=False,
    )
```

```python
import functools

import jax
import jax.numpy as jnp
from jax import lax
from jax.experimental import pallas as pl
from jax.experimental.pallas import tpu as pltpu
from jax.sharding import PartitionSpec as P

F32 = jnp.float32
BF16 = jnp.bfloat16
NEG = -1e30
SIDE = 4


def dot(a, b, ca=1, cb=0):
    return lax.dot_general(a, b, (((ca,), (cb,)), ((), ())), preferred_element_type=F32)


def call(kernel, outs, name, scratch=(), scalars=0, flops=0, nbytes=0):
    vmem = pl.BlockSpec(memory_space=pltpu.VMEM)

    def run(*args):
        specs = [pl.BlockSpec(memory_space=pltpu.SMEM)] * scalars + [vmem] * (len(args) - scalars)
        return pl.pallas_call(
            kernel,
            out_shape=outs,
            in_specs=specs,
            out_specs=jax.tree.map(lambda _: vmem, outs),
            scratch_shapes=list(scratch),
            compiler_params=pltpu.CompilerParams(vmem_limit_bytes=56 * 1024 * 1024),
            cost_estimate=pl.CostEstimate(flops=flops, bytes_accessed=nbytes, transcendentals=0),
            name=name,
        )(*args)

    return run


def scan_lanes(x, reverse=False):
    n = x.shape[1]
    lane = lax.broadcasted_iota(jnp.int32, x.shape, 1)
    k = 1
    while k < n:
        if reverse:
            x = x + jnp.where(lane < n - k, pltpu.roll(x, n - k, 1), 0.0)
        else:
            x = x + jnp.where(lane >= k, pltpu.roll(x, k, 1), 0.0)
        k *= 2
    return x


def prep_kernel(pos, d_ref, z1, z2, z3, x1, x2, x3, oz, ox):
    dp, x, z, core = pos[0], pos[1], pos[2], pos[3]

    def column(d, xx, zz):
        at = (d * SIDE + lax.rem(xx, SIDE)) * SIDE + lax.rem(zz, SIDE)
        return d_ref[:, pl.ds(pl.multiple_of(at * 128, 128), 128)]

    mine = lax.rem(dp + core, 2)
    for k, (zr, xr) in enumerate(((z1, x1), (z2, x2), (z3, x3)), 1):
        for r in range(SIDE):
            cols = slice(r * 128, (r + 1) * 128)
            zr[:, cols] = column(mine, x + r, z + k).astype(F32)
            xr[:, cols] = column(mine, x + k, z + r).astype(F32)
    for kd in range(2):
        d = lax.rem(dp + kd, 2)
        for r in range(SIDE):
            cols = slice(r * 128, (r + 1) * 128)
            oz[kd, :, cols] = column(d, x + r, z)
            ox[kd, :, cols] = column(d, x, z + r)


def ends_kernel(ut_ref, v_ref, b_ref, c_ref, s_ref, r_ref, vt_ref, end_ref, run_ref, *, length):
    heads, tokens = s_ref.shape
    width = v_ref.shape[1] // heads
    run = scan_lanes(s_ref[...] * (r_ref[...] * (-1.0 / length)))
    run_ref[...] = run
    last = run[:, tokens - 1 :]
    grow = jnp.exp(run)
    tail = jnp.exp(last - run) * s_ref[...]
    total = jnp.exp(last)
    b = b_ref[...]
    c = c_ref[...]
    per = 128 // width
    for h in range(0, heads, per):
        vt = v_ref[:, h * width : (h + per) * width].astype(F32).T
        vt_ref[h * width : (h + per) * width, :] = vt.astype(BF16)
        for k in range(per):
            at = h + k
            scaled = vt[k * width : (k + 1) * width] * tail[at : at + 1]
            end_ref[at, :width, :] = dot(scaled.astype(BF16), b)
            scaled = ut_ref[at * width : (at + 1) * width, :].astype(F32) * grow[at : at + 1]
            end_ref[at, width : 2 * width, :] = dot(scaled.astype(BF16), c)
            end_ref[at, 2 * width :, :] = jnp.broadcast_to(total[at : at + 1], (8, 128))


def across_kernel(e_ref, o_ref):
    shards, rows, _ = o_ref.shape
    width = rows // 2
    state = jnp.zeros((width, o_ref.shape[2]), F32)
    for k in range(shards):
        o_ref[k, :width, :] = state
        if k < shards - 1:
            state = state * e_ref[k, rows : rows + 1, :] + e_ref[k, :width, :]
    state = jnp.zeros((width, o_ref.shape[2]), F32)
    for k in reversed(range(shards)):
        o_ref[k, width:, :] = state
        if k:
            state = state * e_ref[k, rows : rows + 1, :] + e_ref[k, width:rows, :]


def columns_of(run, wide_ref):
    heads, tokens = run.shape
    turned = jnp.concatenate([run, jnp.zeros((128 - heads, tokens), F32)], 0).T
    for h in range(heads):
        wide_ref[h] = jnp.broadcast_to(turned[:, h : h + 1], (tokens, 128))


def weights_of(wide, row, steps, tokens):
    i = lax.broadcasted_iota(jnp.int32, (tokens, tokens), 0)
    j = lax.broadcasted_iota(jnp.int32, (tokens, tokens), 1)
    between = jnp.concatenate([wide] * (tokens // 128), 1) - row
    return jnp.exp(jnp.where(i >= j, between, NEG)) * steps


def inside_kernel(g_ref, vt_ref, b_ref, c_ref, s_ref, run_ref, o_ref, wide_ref, g2_ref):
    heads, tokens = s_ref.shape
    width = vt_ref.shape[0] // heads
    columns_of(run_ref[...], wide_ref)
    g2_ref[...] = dot(c_ref[...], b_ref[...], 1, 1)

    def head(h, _):
        row = run_ref[pl.ds(h, 1), :]
        mix = (weights_of(wide_ref[h], row, s_ref[pl.ds(h, 1), :], tokens) * g2_ref[...]).astype(BF16)
        at = pl.ds(pl.multiple_of(h * width, width), width)
        v = vt_ref[at, :]
        o_ref[at, :] = dot(v, mix, 1, 1) + g_ref[h] * v.astype(F32)

    lax.fori_loop(0, heads, head, None, unroll=2)


def mix_kernel(in_ref, c_ref, run_ref, st_ref, ma_ref, mb_ref):
    heads = run_ref.shape[0]
    width = in_ref.shape[0] // heads
    half = heads // 2
    c = c_ref[...]
    for h in range(heads):
        carried = dot(st_ref[h, :width, :].astype(BF16), c, 1, 1) * jnp.exp(run_ref[h : h + 1, :])
        out_ref, to = (ma_ref, h) if h < half else (mb_ref, h - half)
        out_ref[to * width : (to + 1) * width, :] = in_ref[h * width : (h + 1) * width, :] + carried


def back_kernel(
    g_ref, ut_ref, vt_ref, b_ref, c_ref, s_ref, run_ref, r_ref, st_ref, ma_ref, mb_ref,
    dv_ref, dbc_ref, ds_ref, small_ref,
    wide_ref, g2_ref, ct_ref, bt_ref, ue_ref, vw_ref, r1_ref, q_ref, add_ref, skip_ref, dbt_ref, dct_ref, dvt_ref,
    *, length,
):
    heads, tokens = s_ref.shape
    width = vt_ref.shape[0] // heads
    half = heads // 2
    columns_of(run_ref[...], wide_ref)
    g2_ref[...] = dot(c_ref[...], b_ref[...], 1, 1)
    ct_ref[...] = c_ref[...].astype(F32).T.astype(BF16)
    bt_ref[...] = b_ref[...].astype(F32).T.astype(BF16)
    dbt_ref[...] = jnp.zeros_like(dbt_ref)
    dct_ref[...] = jnp.zeros_like(dct_ref)

    def head(h, mixed_ref, base):
        row = run_ref[pl.ds(h, 1), :]
        steps = s_ref[pl.ds(h, 1), :]
        last = row[:, tokens - 1 :]
        at = pl.ds(pl.multiple_of(h * width, width), width)
        v, u = vt_ref[at, :], ut_ref[at, :]
        vf, uf = v.astype(F32), u.astype(F32)
        weights = weights_of(wide_ref[h], row, steps, tokens)
        mix = (weights * g2_ref[...]).astype(BF16)
        pair = dot(u, v, 0, 0)
        dg = (pair * weights).astype(BF16)
        dct_ref[...] += dot(bt_ref[...], dg, 1, 1)
        dbt_ref[...] += dot(ct_ref[...], dg, 1, 0)
        tail = jnp.exp(last - row) * steps
        ue_ref[at, :] = (uf * jnp.exp(row)).astype(BF16)
        vw_ref[at, :] = (vf * tail).astype(BF16)
        gs = st_ref[h, width:, :]
        far = dot(gs.astype(BF16), bt_ref[...]) * tail
        near = dot(u, mix)
        both = near + far
        gain = g_ref[h]
        dvt_ref[at, :] = both + gain * uf
        out = mixed_ref[pl.ds(pl.multiple_of((h - base) * width, width), width), :] - gain * vf
        r1_ref[pl.ds(h, 1), :] = jnp.sum(uf * out, 0, keepdims=True)
        q_ref[pl.ds(h, 1), :] = jnp.sum(vf * both, 0, keepdims=True)
        kept = jnp.sum(st_ref[h, :width, :] * gs, 0, keepdims=True) * jnp.exp(last)
        add_ref[pl.ds(h, 1), :] = jnp.sum(vf * far, 0, keepdims=True) + jnp.concatenate(
            [kept, jnp.zeros((1, tokens - 128), F32)], 1
        )
        skip_ref[pl.ds(h, 1), :] = jnp.sum(uf * vf, 0, keepdims=True)

    lax.fori_loop(0, half, lambda h, _: head(h, ma_ref, 0), None, unroll=2)
    lax.fori_loop(half, heads, lambda h, _: head(h, mb_ref, half), None, unroll=2)

    states = heads * width
    sin_t = st_ref[:, :width, :].reshape(states, 128).T.astype(BF16)
    gs_t = st_ref[:, width:, :].reshape(states, 128).T.astype(BF16)
    dbc_ref[0] = (dbt_ref[...] + dot(gs_t, vw_ref[...])).T
    dbc_ref[1] = (dct_ref[...] + dot(sin_t, ue_ref[...])).T
    for k in range(0, heads * width, 128):
        dv_ref[:, k : k + 128] = dvt_ref[k : k + 128, :].T.astype(BF16)
    dlog = scan_lanes(r1_ref[...] - q_ref[...], reverse=True) + jnp.sum(add_ref[...], 1, keepdims=True)
    s = s_ref[...]
    ds_ref[...] = q_ref[...] / s - dlog * (r_ref[...] * (1.0 / length))
    rates = jnp.sum(s * dlog, 1, keepdims=True) * (-1.0 / length)
    skips = jnp.sum(skip_ref[...], 1, keepdims=True)
    lane = lax.broadcasted_iota(jnp.int32, (heads, 128), 1)
    head_of = lax.broadcasted_iota(jnp.int32, (heads, 128), 0)
    packed = jnp.where(lane == head_of, rates, jnp.where(lane == head_of + heads, skips, 0.0))
    small_ref[...] = jnp.sum(packed, 0, keepdims=True)


def grad_w_kernel(core, m0, m1, m2, m3, own, d1, d2, d3, e1, e2, e3, o0, o1, o2, o3):
    outs = (o0, o1, o2, o3)
    ms = [m[...].astype(BF16) for m in (m0, m1, m2, m3)]
    ds = ((d1, d2, d3), (e1, e2, e3))
    me = core[0]
    for kd in range(2):
        at = me if kd == 0 else 1 - me
        acc = dot(ms[0], own[at])
        for k in range(3):
            acc += dot(ms[k + 1], ds[kd][k][...].astype(BF16))
        for r in range(SIDE):
            outs[r][at] = acc[:, r * 128 : (r + 1) * 128]


def gather_sum_kernel(a0, a1, a2, a3, keep_ref, send_ref):
    keep_ref[...] = a0[0] + a1[0] + a2[0] + a3[0]
    send_ref[...] = a0[1] + a1[1] + a2[1] + a3[1]


def finish_kernel(a0, a1, b0, b1, o_ref):
    n = a0.shape[0]
    o_ref[:, :n] = (a0[...] + a1[...]).T
    o_ref[:, n:] = (b0[...] + b1[...]).T


def body(values, b_proj, c_proj, step_sizes, decay_rates, skip_gain, w_out, d_out):
    tokens, channels = values.shape[1:]
    state = b_proj.shape[2]
    heads = decay_rates.shape[0]
    width = channels // heads
    shards = lax.axis_size("ctx")
    length = tokens * shards
    half = channels // 2
    sds = jax.ShapeDtypeStruct

    place = lax.axis_index("ctx")
    dp = lax.axis_index("dp")
    core = lax.rem(lax.axis_index("tensor"), 2)
    pos = jnp.stack([dp, place // SIDE, lax.rem(place, SIDE), core]).astype(jnp.int32)

    def shift(value, dx, dz):
        pairs = [
            (x * SIDE + z, ((x + dx) % SIDE) * SIDE + (z + dz) % SIDE)
            for x in range(SIDE)
            for z in range(SIDE)
        ]
        return lax.ppermute(value, "ctx", pairs)

    def other_core(value):
        return lax.ppermute(value, "tensor", [(0, 1), (1, 0), (2, 3), (3, 2)])

    def other_chip(value):
        return lax.ppermute(value, "tensor", [(0, 2), (2, 0), (1, 3), (3, 1)])

    def other_dp(value):
        return lax.ppermute(value, "dp", [(0, 1), (1, 0)])

    def spread(value):
        return lax.all_to_all(value, "ctx", 0, 0, tiled=True)

    v, b, c, steps, cot = values[0], b_proj[0], c_proj[0], step_sizes[0], d_out[0]
    rates = decay_rates[:, None]

    def later(value, *first):
        return lax.optimization_barrier((value,) + first)[0]

    piece = sds((tokens, 4 * 128), F32)
    own = sds((2, tokens, 4 * 128), BF16)
    z1, z2, z3, x1, x2, x3, own_z, own_x = call(
        prep_kernel, (piece,) * 6 + (own, own), "prep", scalars=1, nbytes=7 << 20
    )(pos, cot)
    z3, x3, z1, x1 = shift(z3, 0, 3), shift(x3, 3, 0), shift(z1, 0, 1), shift(x1, 1, 0)

    up_t = lax.dot_general(w_out, later(cot, own_z), (((0,), (1,)), ((), ())), preferred_element_type=F32).astype(BF16)
    vt, ends, run = call(
        functools.partial(ends_kernel, length=length),
        (sds((channels, tokens), BF16), sds((heads, 2 * width + 8, state), F32), sds((heads, tokens), F32)),
        "ends",
        nbytes=4 << 20,
        flops=1 << 27,
    )(up_t, v, b, c, steps, rates)
    z2, x2 = shift(later(z2, run), 0, 2), shift(later(x2, run), 2, 0)
    ends = later(ends, z1, z3, x1, x3)
    across = call(across_kernel, sds((shards, 2 * width, state), F32), "across", nbytes=2 << 20)(spread(ends))
    states = spread(across)

    wide = pltpu.VMEM((heads, tokens, 128), F32)
    square = pltpu.VMEM((tokens, tokens), F32)
    inside = call(
        inside_kernel, sds((channels, tokens), F32), "inside", (wide, square), scalars=1, nbytes=4 << 20, flops=1 << 28
    )(skip_gain, vt, b, c, steps, later(run, across))
    swapped = [other_core(p) for p in lax.optimization_barrier((z1, z2, z3, x1, x3, inside, x2))[:5]]
    mixed_a, mixed_b = call(mix_kernel, (sds((half, tokens), F32),) * 2, "mix", nbytes=4 << 20, flops=1 << 27)(
        inside, c, run, states
    )
    mixed_a, mixed_b, *swapped = lax.optimization_barrier((mixed_a, mixed_b, *swapped))
    sent = [z1, z2, z3, x1, x2, x3]
    b1, b3 = shift(mixed_b, 1, 0), shift(mixed_b, 3, 0)
    a1, a3, a2 = shift(mixed_a, 0, 1), shift(mixed_a, 0, 3), shift(mixed_a, 0, 2)

    dv, dbc, dsteps, small = call(
        functools.partial(back_kernel, length=length),
        (
            sds((tokens, channels), BF16),
            sds((2, tokens, state), F32),
            sds((heads, tokens), F32),
            sds((1, 128), F32),
        ),
        "back",
        (
            wide, square, pltpu.VMEM((state, tokens), BF16), pltpu.VMEM((state, tokens), BF16),
            pltpu.VMEM((channels, tokens), BF16), pltpu.VMEM((channels, tokens), BF16),
            pltpu.VMEM((heads, tokens), F32), pltpu.VMEM((heads, tokens), F32),
            pltpu.VMEM((heads, tokens), F32), pltpu.VMEM((heads, tokens), F32),
            pltpu.VMEM((state, tokens), F32), pltpu.VMEM((state, tokens), F32),
            pltpu.VMEM((channels, tokens), F32),
        ),
        scalars=1,
        flops=1 << 30,
        nbytes=6 << 20,
    )(skip_gain, up_t, vt, b, c, steps, run, rates, states, mixed_a, mixed_b)

    b2 = shift(later(mixed_b, b1, b3, small), 2, 0)
    small = later(small, b1, b3)
    small = spread(jnp.broadcast_to(small[None], (shards,) + small.shape)).sum(0)
    swapped.insert(4, other_core(later(x2, small)))

    out = (sds((2, half, 128), F32),) * 4
    flops = 2 * half * 4 * tokens * 1024
    me = core[None].astype(jnp.int32)
    pa = call(grad_w_kernel, out, "grad_w_a", scalars=1, flops=flops, nbytes=8 << 20)(
        me, later(mixed_a, small), a1, a2, a3, own_z, *sent[:3], *swapped[:3]
    )
    ra = [pa[0]] + [shift(pa[k], k, 0) for k in range(1, SIDE)]
    pb = call(grad_w_kernel, out, "grad_w_b", scalars=1, flops=flops, nbytes=8 << 20)(
        me, later(mixed_b, pa[0]), b1, b2, b3, own_x, *sent[3:], *swapped[3:]
    )
    rb = [pb[0]] + [shift(pb[k], 0, k) for k in range(1, SIDE)]

    dbc = later(dbc, pa[0])
    dbc = dbc + other_core(dbc)
    dbc = dbc + other_chip(dbc)
    small = small + other_dp(small)

    pair = (sds((half, 128), F32),) * 2
    kept_a, away_a = call(gather_sum_kernel, pair, "gather_sum_a", nbytes=3 << 20)(*ra)
    away_a = other_dp(away_a)
    kept_b, away_b = call(gather_sum_kernel, pair, "gather_sum_b", nbytes=3 << 20)(*rb)
    away_b = other_dp(away_b)
    d_w = call(finish_kernel, sds((128, channels), F32), "finish", nbytes=2 << 20)(kept_a, away_a, kept_b, away_b)
    return (dv[None], dbc[0][None], dbc[1][None], dsteps[None], small[0, :heads], small[0, heads : 2 * heads], d_w)


def solution(mesh):
    return jax.shard_map(
        body,
        mesh=mesh,
        in_specs=(
            P("dp", "ctx", "tensor"),
            P("dp", "ctx", None),
            P("dp", "ctx", None),
            P("dp", "tensor", "ctx"),
            P("tensor"),
            P("tensor"),
            P(None, "tensor"),
            P("dp", "ctx", None),
        ),
        out_specs=(
            P("dp", "ctx", "tensor"),
            P("dp", "ctx", None),
            P("dp", "ctx", None),
            P("dp", "tensor", "ctx"),
            P("tensor"),
            P("tensor"),
            P(("dp", "ctx"), "tensor"),
        ),
        check_vma=False,
    )
```

```python
import functools

import jax
import jax.numpy as jnp
from jax import lax
from jax.experimental import pallas as pl
from jax.experimental.pallas import tpu as pltpu
from jax.sharding import PartitionSpec as P

F32 = jnp.float32
BF16 = jnp.bfloat16
NEG = -1e30
SIDE = 4


def dot(a, b, ca=1, cb=0):
    return lax.dot_general(a, b, (((ca,), (cb,)), ((), ())), preferred_element_type=F32)


def call(kernel, outs, name, scratch=(), scalars=0, flops=0, nbytes=0):
    vmem = pl.BlockSpec(memory_space=pltpu.VMEM)

    def run(*args):
        specs = [pl.BlockSpec(memory_space=pltpu.SMEM)] * scalars + [vmem] * (len(args) - scalars)
        return pl.pallas_call(
            kernel,
            out_shape=outs,
            in_specs=specs,
            out_specs=jax.tree.map(lambda _: vmem, outs),
            scratch_shapes=list(scratch),
            compiler_params=pltpu.CompilerParams(vmem_limit_bytes=56 * 1024 * 1024),
            cost_estimate=pl.CostEstimate(flops=flops, bytes_accessed=nbytes, transcendentals=0),
            name=name,
        )(*args)

    return run


def scan_lanes(x, reverse=False):
    n = x.shape[1]
    lane = lax.broadcasted_iota(jnp.int32, x.shape, 1)
    k = 1
    while k < n:
        if reverse:
            x = x + jnp.where(lane < n - k, pltpu.roll(x, n - k, 1), 0.0)
        else:
            x = x + jnp.where(lane >= k, pltpu.roll(x, k, 1), 0.0)
        k *= 2
    return x


def piece_of(pos, d_ref):
    dp, x, z, core = pos[0], pos[1], pos[2], pos[3]

    def column(d, dx, dz):
        at = (d * SIDE + lax.rem(x + dx, SIDE)) * SIDE + lax.rem(z + dz, SIDE)
        return d_ref[:, pl.ds(pl.multiple_of(at * 128, 128), 128)]

    return column, dp, lax.rem(dp + core, 2)


def near_kernel(pos, d_ref, z1, z3, x1, x3):
    column, _, mine = piece_of(pos, d_ref)
    for k, zr, xr in ((1, z1, x1), (3, z3, x3)):
        for r in range(SIDE):
            cols = slice(r * 128, (r + 1) * 128)
            zr[:, cols] = column(mine, r, k).astype(F32)
            xr[:, cols] = column(mine, k, r).astype(F32)


def far_kernel(pos, d_ref, z2, x2, oz, ox):
    column, dp, mine = piece_of(pos, d_ref)
    for r in range(SIDE):
        cols = slice(r * 128, (r + 1) * 128)
        z2[:, cols] = column(mine, r, 2).astype(F32)
        x2[:, cols] = column(mine, 2, r).astype(F32)
        for kd in range(2):
            d = lax.rem(dp + kd, 2)
            oz[kd, :, cols] = column(d, r, 0)
            ox[kd, :, cols] = column(d, 0, r)


def ends_kernel(ut_ref, v_ref, b_ref, c_ref, s_ref, r_ref, vt_ref, end_ref, run_ref, *, length):
    heads, tokens = s_ref.shape
    width = v_ref.shape[1] // heads
    run = scan_lanes(s_ref[...] * (r_ref[...] * (-1.0 / length)))
    run_ref[...] = run
    last = run[:, tokens - 1 :]
    grow = jnp.exp(run)
    tail = jnp.exp(last - run) * s_ref[...]
    total = jnp.exp(last)
    b = b_ref[...]
    c = c_ref[...]
    per = 128 // width
    for h in range(0, heads, per):
        vt = v_ref[:, h * width : (h + per) * width].astype(F32).T
        vt_ref[h * width : (h + per) * width, :] = vt.astype(BF16)
        for k in range(per):
            at = h + k
            scaled = vt[k * width : (k + 1) * width] * tail[at : at + 1]
            end_ref[at, :width, :] = dot(scaled.astype(BF16), b)
            scaled = ut_ref[at * width : (at + 1) * width, :].astype(F32) * grow[at : at + 1]
            end_ref[at, width : 2 * width, :] = dot(scaled.astype(BF16), c)
            end_ref[at, 2 * width :, :] = jnp.broadcast_to(total[at : at + 1], (8, 128))


def across_kernel(e_ref, o_ref):
    shards, rows, _ = o_ref.shape
    width = rows // 2
    state = jnp.zeros((width, o_ref.shape[2]), F32)
    for k in range(shards):
        o_ref[k, :width, :] = state
        if k < shards - 1:
            state = state * e_ref[k, rows : rows + 1, :] + e_ref[k, :width, :]
    state = jnp.zeros((width, o_ref.shape[2]), F32)
    for k in reversed(range(shards)):
        o_ref[k, width:, :] = state
        if k:
            state = state * e_ref[k, rows : rows + 1, :] + e_ref[k, width:rows, :]


def columns_of(run, wide_ref):
    heads, tokens = run.shape
    turned = jnp.concatenate([run, jnp.zeros((128 - heads, tokens), F32)], 0).T
    for h in range(heads):
        wide_ref[h] = jnp.broadcast_to(turned[:, h : h + 1], (tokens, 128))


def weights_of(wide, row, steps, tokens):
    i = lax.broadcasted_iota(jnp.int32, (tokens, tokens), 0)
    j = lax.broadcasted_iota(jnp.int32, (tokens, tokens), 1)
    between = jnp.concatenate([wide] * (tokens // 128), 1) - row
    return jnp.exp(jnp.where(i >= j, between, NEG)) * steps


def inside_kernel(g_ref, vt_ref, b_ref, c_ref, s_ref, run_ref, o_ref, wide_ref, g2_ref):
    heads, tokens = s_ref.shape
    width = vt_ref.shape[0] // heads
    columns_of(run_ref[...], wide_ref)
    g2_ref[...] = dot(c_ref[...], b_ref[...], 1, 1)

    def head(h, _):
        row = run_ref[pl.ds(h, 1), :]
        mix = (weights_of(wide_ref[h], row, s_ref[pl.ds(h, 1), :], tokens) * g2_ref[...]).astype(BF16)
        at = pl.ds(pl.multiple_of(h * width, width), width)
        v = vt_ref[at, :]
        o_ref[at, :] = dot(v, mix, 1, 1) + g_ref[h] * v.astype(F32)

    lax.fori_loop(0, heads, head, None, unroll=2)


def mix_kernel(in_ref, c_ref, run_ref, st_ref, ma_ref, mb_ref):
    heads = run_ref.shape[0]
    width = in_ref.shape[0] // heads
    half = heads // 2
    c = c_ref[...]
    for h in range(heads):
        carried = dot(st_ref[h, :width, :].astype(BF16), c, 1, 1) * jnp.exp(run_ref[h : h + 1, :])
        out_ref, to = (ma_ref, h) if h < half else (mb_ref, h - half)
        out_ref[to * width : (to + 1) * width, :] = in_ref[h * width : (h + 1) * width, :] + carried


def back_kernel(
    g_ref, ut_ref, vt_ref, b_ref, c_ref, s_ref, run_ref, r_ref, st_ref, ma_ref, mb_ref,
    dv_ref, dbc_ref, ds_ref, small_ref,
    wide_ref, g2_ref, ct_ref, bt_ref, ue_ref, vw_ref, r1_ref, q_ref, add_ref, skip_ref, dbt_ref, dct_ref, dvt_ref,
    *, length,
):
    heads, tokens = s_ref.shape
    width = vt_ref.shape[0] // heads
    half = heads // 2
    columns_of(run_ref[...], wide_ref)
    g2_ref[...] = dot(c_ref[...], b_ref[...], 1, 1)
    ct_ref[...] = c_ref[...].astype(F32).T.astype(BF16)
    bt_ref[...] = b_ref[...].astype(F32).T.astype(BF16)
    dbt_ref[...] = jnp.zeros_like(dbt_ref)
    dct_ref[...] = jnp.zeros_like(dct_ref)

    def head(h, mixed_ref, base):
        row = run_ref[pl.ds(h, 1), :]
        steps = s_ref[pl.ds(h, 1), :]
        last = row[:, tokens - 1 :]
        at = pl.ds(pl.multiple_of(h * width, width), width)
        v, u = vt_ref[at, :], ut_ref[at, :]
        vf, uf = v.astype(F32), u.astype(F32)
        weights = weights_of(wide_ref[h], row, steps, tokens)
        mix = (weights * g2_ref[...]).astype(BF16)
        pair = dot(u, v, 0, 0)
        dg = (pair * weights).astype(BF16)
        dct_ref[...] += dot(bt_ref[...], dg, 1, 1)
        dbt_ref[...] += dot(ct_ref[...], dg, 1, 0)
        tail = jnp.exp(last - row) * steps
        ue_ref[at, :] = (uf * jnp.exp(row)).astype(BF16)
        vw_ref[at, :] = (vf * tail).astype(BF16)
        gs = st_ref[h, width:, :]
        far = dot(gs.astype(BF16), bt_ref[...]) * tail
        near = dot(u, mix)
        both = near + far
        gain = g_ref[h]
        dvt_ref[at, :] = both + gain * uf
        out = mixed_ref[pl.ds(pl.multiple_of((h - base) * width, width), width), :] - gain * vf
        r1_ref[pl.ds(h, 1), :] = jnp.sum(uf * out, 0, keepdims=True)
        q_ref[pl.ds(h, 1), :] = jnp.sum(vf * both, 0, keepdims=True)
        kept = jnp.sum(st_ref[h, :width, :] * gs, 0, keepdims=True) * jnp.exp(last)
        add_ref[pl.ds(h, 1), :] = jnp.sum(vf * far, 0, keepdims=True) + jnp.concatenate(
            [kept, jnp.zeros((1, tokens - 128), F32)], 1
        )
        skip_ref[pl.ds(h, 1), :] = jnp.sum(uf * vf, 0, keepdims=True)

    lax.fori_loop(0, half, lambda h, _: head(h, ma_ref, 0), None, unroll=2)
    lax.fori_loop(half, heads, lambda h, _: head(h, mb_ref, half), None, unroll=2)

    states = heads * width
    sin_t = st_ref[:, :width, :].reshape(states, 128).T.astype(BF16)
    gs_t = st_ref[:, width:, :].reshape(states, 128).T.astype(BF16)
    dbc_ref[0] = (dbt_ref[...] + dot(gs_t, vw_ref[...])).T
    dbc_ref[1] = (dct_ref[...] + dot(sin_t, ue_ref[...])).T
    for k in range(0, heads * width, 128):
        dv_ref[:, k : k + 128] = dvt_ref[k : k + 128, :].T.astype(BF16)
    dlog = scan_lanes(r1_ref[...] - q_ref[...], reverse=True) + jnp.sum(add_ref[...], 1, keepdims=True)
    s = s_ref[...]
    ds_ref[...] = q_ref[...] / s - dlog * (r_ref[...] * (1.0 / length))
    rates = jnp.sum(s * dlog, 1, keepdims=True) * (-1.0 / length)
    skips = jnp.sum(skip_ref[...], 1, keepdims=True)
    lane = lax.broadcasted_iota(jnp.int32, (heads, 128), 1)
    head_of = lax.broadcasted_iota(jnp.int32, (heads, 128), 0)
    packed = jnp.where(lane == head_of, rates, jnp.where(lane == head_of + heads, skips, 0.0))
    small_ref[...] = jnp.sum(packed, 0, keepdims=True)


def grad_w_kernel(core, m0, m1, m2, m3, own, d1, d2, d3, e1, e2, e3, o0, o1, o2, o3):
    outs = (o0, o1, o2, o3)
    ms = [m[...].astype(BF16) for m in (m0, m1, m2, m3)]
    ds = ((d1, d2, d3), (e1, e2, e3))
    me = core[0]
    for kd in range(2):
        at = me if kd == 0 else 1 - me
        acc = dot(ms[0], own[at])
        for k in range(3):
            acc += dot(ms[k + 1], ds[kd][k][...].astype(BF16))
        for r in range(SIDE):
            outs[r][at] = acc[:, r * 128 : (r + 1) * 128]


def gather_sum_kernel(a0, a1, a2, a3, keep_ref, send_ref):
    keep_ref[...] = a0[0] + a1[0] + a2[0] + a3[0]
    send_ref[...] = a0[1] + a1[1] + a2[1] + a3[1]


def finish_kernel(a0, a1, b0, b1, o_ref):
    n = a0.shape[0]
    o_ref[:, :n] = (a0[...] + a1[...]).T
    o_ref[:, n:] = (b0[...] + b1[...]).T


def body(values, b_proj, c_proj, step_sizes, decay_rates, skip_gain, w_out, d_out):
    tokens, channels = values.shape[1:]
    state = b_proj.shape[2]
    heads = decay_rates.shape[0]
    width = channels // heads
    shards = lax.axis_size("ctx")
    length = tokens * shards
    half = channels // 2
    sds = jax.ShapeDtypeStruct

    place = lax.axis_index("ctx")
    dp = lax.axis_index("dp")
    core = lax.rem(lax.axis_index("tensor"), 2)
    pos = jnp.stack([dp, place // SIDE, lax.rem(place, SIDE), core]).astype(jnp.int32)

    def shift(value, dx, dz):
        pairs = [
            (x * SIDE + z, ((x + dx) % SIDE) * SIDE + (z + dz) % SIDE)
            for x in range(SIDE)
            for z in range(SIDE)
        ]
        return lax.ppermute(value, "ctx", pairs)

    def other_core(value):
        return lax.ppermute(value, "tensor", [(0, 1), (1, 0), (2, 3), (3, 2)])

    def other_chip(value):
        return lax.ppermute(value, "tensor", [(0, 2), (2, 0), (1, 3), (3, 1)])

    def other_dp(value):
        return lax.ppermute(value, "dp", [(0, 1), (1, 0)])

    def spread(value):
        return lax.all_to_all(value, "ctx", 0, 0, tiled=True)

    v, b, c, steps, cot = values[0], b_proj[0], c_proj[0], step_sizes[0], d_out[0]
    rates = decay_rates[:, None]

    def later(value, *first):
        return lax.optimization_barrier((value,) + first)[0]

    piece = sds((tokens, 4 * 128), F32)
    own = sds((2, tokens, 4 * 128), BF16)
    z1, z3, x1, x3 = call(near_kernel, (piece,) * 4, "near", scalars=1, nbytes=4 << 20)(pos, cot)
    placed = later(cot, z1)
    z3, x3, z1, x1 = shift(z3, 0, 3), shift(x3, 3, 0), shift(z1, 0, 1), shift(x1, 1, 0)

    up_t = lax.dot_general(w_out, placed, (((0,), (1,)), ((), ())), preferred_element_type=F32).astype(BF16)
    vt, ends, run = call(
        functools.partial(ends_kernel, length=length),
        (sds((channels, tokens), BF16), sds((heads, 2 * width + 8, state), F32), sds((heads, tokens), F32)),
        "ends",
        nbytes=4 << 20,
        flops=1 << 27,
    )(up_t, v, b, c, steps, rates)
    z2, x2, own_z, own_x = call(far_kernel, (piece, piece, own, own), "far", scalars=1, nbytes=5 << 20)(
        pos, later(cot, run)
    )
    z2, x2 = shift(z2, 0, 2), shift(x2, 2, 0)
    ends = later(ends, z1, z3, x1, x3)
    across = call(across_kernel, sds((shards, 2 * width, state), F32), "across", nbytes=2 << 20)(spread(ends))
    states = spread(across)

    wide = pltpu.VMEM((heads, tokens, 128), F32)
    square = pltpu.VMEM((tokens, tokens), F32)
    inside = call(
        inside_kernel, sds((channels, tokens), F32), "inside", (wide, square), scalars=1, nbytes=4 << 20, flops=1 << 28
    )(skip_gain, vt, b, c, steps, later(run, across))
    swapped = [other_core(p) for p in lax.optimization_barrier((z1, z2, z3, x1, x3, inside, x2))[:5]]
    mixed_a, mixed_b = call(mix_kernel, (sds((half, tokens), F32),) * 2, "mix", nbytes=4 << 20, flops=1 << 27)(
        inside, c, run, states
    )
    mixed_a, mixed_b, *swapped = lax.optimization_barrier((mixed_a, mixed_b, *swapped))
    sent = [z1, z2, z3, x1, x2, x3]
    b1, b3 = shift(mixed_b, 1, 0), shift(mixed_b, 3, 0)
    a1, a3, a2 = shift(mixed_a, 0, 1), shift(mixed_a, 0, 3), shift(mixed_a, 0, 2)

    dv, dbc, dsteps, small = call(
        functools.partial(back_kernel, length=length),
        (
            sds((tokens, channels), BF16),
            sds((2, tokens, state), F32),
            sds((heads, tokens), F32),
            sds((1, 128), F32),
        ),
        "back",
        (
            wide, square, pltpu.VMEM((state, tokens), BF16), pltpu.VMEM((state, tokens), BF16),
            pltpu.VMEM((channels, tokens), BF16), pltpu.VMEM((channels, tokens), BF16),
            pltpu.VMEM((heads, tokens), F32), pltpu.VMEM((heads, tokens), F32),
            pltpu.VMEM((heads, tokens), F32), pltpu.VMEM((heads, tokens), F32),
            pltpu.VMEM((state, tokens), F32), pltpu.VMEM((state, tokens), F32),
            pltpu.VMEM((channels, tokens), F32),
        ),
        scalars=1,
        flops=1 << 30,
        nbytes=6 << 20,
    )(skip_gain, up_t, vt, b, c, steps, run, rates, states, mixed_a, mixed_b)

    b2 = shift(later(mixed_b, b1, b3, small), 2, 0)
    small = later(small, b1, b3)
    small = spread(jnp.broadcast_to(small[None], (shards,) + small.shape)).sum(0)
    swapped.insert(4, other_core(later(x2, small)))

    out = (sds((2, half, 128), F32),) * 4
    flops = 2 * half * 4 * tokens * 1024
    me = core[None].astype(jnp.int32)
    pa = call(grad_w_kernel, out, "grad_w_a", scalars=1, flops=flops, nbytes=8 << 20)(
        me, later(mixed_a, small), a1, a2, a3, own_z, *sent[:3], *swapped[:3]
    )
    ra = [pa[0]] + [shift(pa[k], k, 0) for k in range(1, SIDE)]
    pb = call(grad_w_kernel, out, "grad_w_b", scalars=1, flops=flops, nbytes=8 << 20)(
        me, later(mixed_b, pa[0]), b1, b2, b3, own_x, *sent[3:], *swapped[3:]
    )
    rb = [pb[0]] + [shift(pb[k], 0, k) for k in range(1, SIDE)]

    dbc = later(dbc, pa[0])
    dbc = dbc + other_core(dbc)
    dbc = dbc + other_chip(dbc)
    small = small + other_dp(small)

    pair = (sds((half, 128), F32),) * 2
    kept_a, away_a = call(gather_sum_kernel, pair, "gather_sum_a", nbytes=3 << 20)(*ra)
    away_a = other_dp(away_a)
    kept_b, away_b = call(gather_sum_kernel, pair, "gather_sum_b", nbytes=3 << 20)(*rb)
    away_b = other_dp(away_b)
    d_w = call(finish_kernel, sds((128, channels), F32), "finish", nbytes=2 << 20)(kept_a, away_a, kept_b, away_b)
    return (dv[None], dbc[0][None], dbc[1][None], dsteps[None], small[0, :heads], small[0, heads : 2 * heads], d_w)


def solution(mesh):
    return jax.shard_map(
        body,
        mesh=mesh,
        in_specs=(
            P("dp", "ctx", "tensor"),
            P("dp", "ctx", None),
            P("dp", "ctx", None),
            P("dp", "tensor", "ctx"),
            P("tensor"),
            P("tensor"),
            P(None, "tensor"),
            P("dp", "ctx", None),
        ),
        out_specs=(
            P("dp", "ctx", "tensor"),
            P("dp", "ctx", None),
            P("dp", "ctx", None),
            P("dp", "tensor", "ctx"),
            P("tensor"),
            P("tensor"),
            P(("dp", "ctx"), "tensor"),
        ),
        check_vma=False,
    )
```
